128 devices in a mesh: section: 2 (over z_hi), seq: 8 (over x, z_lo), expert: 8 (over y, core).
Axes of the slice: x: 4, y: 4, z: 4 (z_hi: 2, z_lo: 2; z = z_hi * 2 + z_lo), core: 2. Of those that a mesh axis runs over, the one named last changes fastest.
Arguments:
- tokens: bfloat16 [2, 1024, 2048], P(None, ('seq', 'expert')), may hold values from -12 to 12
- prompt_lengths: int32 [2, 3], replicated, may hold values from 1 to 512, 1024 in all within a row
- cache_lengths: int32 [2, 3], replicated, may hold values from 1 to 1024, 2048 in all within a row
- kv_cache: bfloat16 [2, 2048, 2, 2048], P(None, 'seq', None, 'expert'), may hold values from -360 to 360
- attn_routes: int32 [2, 1024, 2], P(None, 'seq'), may hold values from 0 to 3, all different within a row
- ffn_routes: int32 [2, 1024, 2], P(None, ('seq', 'expert')), may hold values from 0 to 7, all different within a row; in each aligned block of 16 rows (0 to 15, 16 to 31, ..., all dimensions but the last counted through in order) at most 8 rows name the same one
- attn_gain: float32 [2048], replicated, may hold values from 0.1 to 1.9
- ffn_gain: float32 [2048], replicated, may hold values from 0.1 to 1.9
- attn_mix: bfloat16 [2048, 4], replicated, may hold values from -0.125 to 0.125
- query_weight: bfloat16 [2048, 4, 2048], P(None, None, 'expert'), may hold values from -0.125 to 0.125
- kv_weight: bfloat16 [2048, 2, 2048], P(None, None, 'expert'), may hold values from -0.125 to 0.125
- out_weight: bfloat16 [4, 2048, 2048], P(None, 'expert'), may hold values from -0.125 to 0.125
- ffn_mix: bfloat16 [2048, 8], replicated, may hold values from -0.125 to 0.125
- in_weight: bfloat16 [8, 2048, 2, 5632], P('expert', None, None, 'seq'), may hold values from -0.125 to 0.125
- down_weight: bfloat16 [8, 5632, 2048], P('expert', 'seq'), may hold values from -0.078125 to 0.078125
Outputs:
- layer_out: bfloat16 [2, 1024, 2048], P('section', ('seq', 'expert'))
The draws below stay inside these ranges and needn't reach their ends.
Inputs may be any that keep to these rules, and one draw needn't show every extreme that they name: `prompt_lengths`: each row sums to 1024; its largest entry is 512. `cache_lengths`: each row sums to 2048; its largest entry is 1024. `attn_routes`: the two experts of a position differ; every expert is named somewhere. `ffn_routes`: the two experts of a position differ. Taking all micro-batches and positions in order, in each aligned block of 16 positions (the rows of one device) no expert is named more than 8 times, and some block names one exactly 8 times.
All inputs are finite; a program needn't handle non-finite values.
Results may differ from the reference program's by a relative error of at most 0.029.
Values may be sent and summed in bfloat16 or wider, within the bound.
A program may use at most 128 MiB of HBM per device.

```python
import math
import jax
import jax.numpy as jnp
import numpy as np
from jax import lax

D = 2048
HEADS = 16
HEAD_DIM = 128
ATT_EXPERTS = 4
FF = 5632
MICRO = 2
PROMPTS = 3
EXPERTS = 8
PACK = 1024
CACHE = 2048
ROWS_FFN = 16
CAP = 8
FF_GROUP = 704
N_SEQ = 8


def draw_tokens(key, part):
    first, second, third = jax.random.split(key, 3)
    base = jnp.clip(jax.random.normal(first, (MICRO, PACK, D), jnp.float32), -6.0, 6.0)
    rows = jnp.exp(jax.random.uniform(second, (MICRO, PACK, 1), jnp.float32, math.log(0.1), 0.0))
    columns = jnp.exp(jax.random.uniform(third, (1, 1, D), jnp.float32, -0.69, 0.69))
    return (base * rows * columns).astype(jnp.bfloat16)


def draw_kv_cache(key, part):
    first = jax.random.fold_in(key, 0)
    shape = (MICRO, CACHE, 2, HEADS * HEAD_DIM)
    base = jnp.clip(jax.random.normal(first, shape, jnp.float32), -6.0, 6.0)
    return base.astype(jnp.bfloat16)


def block_scale(own_key, dims, cuts, low, top_value):
    factor_of, own = 1.0, jax.random.fold_in(own_key, 6)
    for axis_at, blocks in cuts:
        heights = jnp.exp(jax.random.uniform(jax.random.fold_in(own, axis_at), (blocks,), jnp.float32, low / len(cuts), top_value / len(cuts)))
        factor_of = factor_of * jnp.repeat(heights, dims[axis_at] // blocks).reshape([-1 if axis == axis_at else 1 for axis in range(len(dims))])
    return factor_of


def different_ones(rng, rows, number_of, top, lift):
    order = jax.random.permutation(jax.random.fold_in(rng, 1), number_of)
    favour = order
    for power in range(3):
        favour = favour * favour // number_of
    favour = favour * lift // number_of
    chance = jax.random.randint(jax.random.fold_in(rng, 2), (rows, number_of), 0, 4096) + favour
    holders = jax.random.permutation(jax.random.fold_in(rng, 3), rows)[jnp.arange(number_of) % rows]
    chance = jnp.where(jnp.arange(rows)[:, None] == holders[None, :], 1 << 14, chance)
    score = chance * number_of + jnp.arange(number_of)
    return lax.top_k(score.astype(jnp.int32), top)[1].astype(jnp.int32)


def profile(number_of, total, most, slope):
    portions = [(1 << 20) // math.isqrt(rank ** slope) + 1 for rank in range(2, number_of + 1)]
    spare, holding = total - most - (number_of - 1), [1] * (number_of - 1)
    while spare > 0:
        free = [i for i in range(number_of - 1) if holding[i] < most]
        pool, budget = sum([portions[i] for i in free]), spare
        for i in free:
            extra = min(most - holding[i], max(1, budget * portions[i] // pool), spare)
            holding[i] = holding[i] + extra
            spare = spare - extra
    return np.array([most] + holding)


def uneven_parts(key, count, total, most, lean):
    if count == 2:
        one = jax.random.randint(key, (), max(1, total - most), min(most, total - 1) + 1)
        return jnp.stack([one, total - one])
    sizes = jnp.asarray(profile(count, total, most, lean), jnp.int32)
    pairs = (count - 1) // 2
    donor, sink = sizes[1:1 + 2 * pairs:2], sizes[2:2 + 2 * pairs:2]
    room = jnp.minimum(donor - 1, most - sink)
    shifted = jax.random.randint(jax.random.fold_in(key, 1), (pairs,), 0, 1 << 20) % (room + 1)
    sizes = sizes.at[1:1 + 2 * pairs:2].set(donor - shifted).at[2:2 + 2 * pairs:2].set(sink + shifted)
    return sizes[jax.random.permutation(jax.random.fold_in(key, 2), count)]


def routed_block(own_key, own, number, rows, number_of, top, reach, slope):
    order = jax.random.permutation(own_key, number_of)
    crowded, ordinary = portions_of(number_of, rows * top, reach, slope, True), portions_of(number_of, rows * top, reach, slope, False)
    places = jnp.arange(number_of)

    def named(sizes, offset_by):
        used = int((sizes > 0).sum())
        fixed = max(1, used // 4)
        passed = fixed + (places - fixed + offset_by * (used - fixed)) % max(1, number_of - fixed)
        return jnp.zeros((number_of,), jnp.int32).at[order[jnp.where(places < fixed, places, passed)]].set(jnp.asarray(sizes, jnp.int32))

    sizes = jnp.where(number % 4 == 0, named(crowded, number // 4), named(ordinary, number - number // 4 - 1))
    mixed = jax.random.permutation(jax.random.fold_in(own, 3), number_of)
    source_of, sink = mixed[0:number_of // 2 * 2:2], mixed[1:number_of // 2 * 2:2]
    slack = jnp.minimum(sizes[source_of] - 1, reach - sizes[sink]) // 2
    slack = jnp.where((source_of == order[0]) | (sink == order[0]) | (sizes[sink] == 0), 0, jnp.maximum(slack, 0))
    passed = jax.random.randint(jax.random.fold_in(own, 4), (number_of // 2,), 0, 1 << 20) % (slack + 1)
    sizes = sizes.at[source_of].add(-passed).at[sink].add(passed)
    members = jnp.searchsorted(jnp.cumsum(sizes), jnp.arange(rows * top), side="right").astype(jnp.int32)
    listing = members.reshape(top, rows).T
    listing = listing[jax.random.permutation(jax.random.fold_in(own, 1), rows)]
    offset_by = jax.random.randint(jax.random.fold_in(own, 2), (rows, 1), 0, top)
    return jnp.take_along_axis(listing, (jnp.arange(top)[None, :] + offset_by) % top, axis=1)


def portions_of(count, total, limit, lean, full):
    weights = [(1 << 20) // math.isqrt(rank ** lean) + 1 for rank in range(1, count + 1)]
    largest = limit if full else min(limit, max(-(-total // count), total * weights[0] // sum(weights)))
    least = 1 if total - largest >= count - 1 else 0
    holding, surplus = [largest] + [least] * (count - 1), total - largest - least * (count - 1)
    while surplus > 0:
        movable = [i for i in range(1, count) if holding[i] < largest] or [i for i in range(1, count) if holding[i] < limit]
        pool, budget = sum([weights[i] for i in movable]), surplus
        for i in movable:
            addition = min(limit - holding[i], max(1, budget * weights[i] // pool), surplus)
            holding[i] = holding[i] + addition
            surplus = surplus - addition
    return np.array(holding)


def normal_values(rng, dims, width, most, cuts=(), kind=jnp.bfloat16):
    values = jax.random.normal(rng, dims, jnp.float32) * width
    if len(cuts) > 0:
        values = block_scale(rng, dims, cuts, -0.22, 0.18) * values
    return jnp.clip(values, min=-most, max=most).astype(kind)


def setup_inputs(seed: int = 0) -> dict:
    splits = jax.random.split(jax.random.key(seed), 16)
    tokens = draw_tokens(jax.random.fold_in(splits[15], 71), 0)
    prompt_lengths = jax.vmap(lambda own: uneven_parts(own, PROMPTS, PACK, PACK // 2, 2))(jax.random.split(splits[1], MICRO)).reshape((MICRO, PROMPTS)).astype(jnp.int32)
    cache_lengths = jax.vmap(lambda own: uneven_parts(own, PROMPTS, CACHE, CACHE // 2, 2))(jax.random.split(splits[2], MICRO)).reshape((MICRO, PROMPTS)).astype(jnp.int32)
    kv_cache = draw_kv_cache(jax.random.fold_in(splits[15], 71), 0)
    attn_routes = different_ones(splits[4], MICRO * PACK, ATT_EXPERTS, 2, 0).reshape((MICRO, PACK, 2))
    ffn_routes_keys = jax.random.split(jax.random.fold_in(splits[5], 1), MICRO * PACK // ROWS_FFN)
    ffn_routes_turns = jax.random.permutation(jax.random.fold_in(splits[5], 3), MICRO * PACK // ROWS_FFN)
    ffn_routes = jax.vmap(lambda own, number: routed_block(jax.random.fold_in(splits[5], 2), own, number, ROWS_FFN, EXPERTS, 2, CAP, 1))(ffn_routes_keys, ffn_routes_turns).reshape((MICRO, PACK, 2))
    attn_gain = jnp.clip(1.0 + 0.18 * jax.random.normal(splits[6], (D,), jnp.float32), 0.1, 1.9)
    ffn_gain = jnp.clip(1.0 + 0.18 * jax.random.normal(splits[7], (D,), jnp.float32), 0.1, 1.9)
    attn_mix = normal_values(splits[8], (D, ATT_EXPERTS), D ** -0.5, 0.125)
    query_weight = normal_values(splits[9], (D, ATT_EXPERTS, HEADS * HEAD_DIM), D ** -0.5, 0.125, ((2, 8),))
    kv_weight = normal_values(splits[10], (D, 2, HEADS * HEAD_DIM), D ** -0.5, 0.125, ((2, 8),))
    out_weight = normal_values(splits[11], (ATT_EXPERTS, HEADS * HEAD_DIM, D), (HEADS * HEAD_DIM) ** -0.5, 0.125, ((1, 8),))
    ffn_mix = normal_values(splits[12], (D, EXPERTS), D ** -0.5, 0.125)
    in_weight = normal_values(splits[13], (EXPERTS, D, 2, FF), D ** -0.5, 0.125, ((0, 8), (3, 8)))
    down_weight = normal_values(splits[14], (EXPERTS, FF, D), FF ** -0.5, 0.078125, ((0, 8), (1, 8)))
    return {"tokens": tokens, "prompt_lengths": prompt_lengths, "cache_lengths": cache_lengths, "kv_cache": kv_cache, "attn_routes": attn_routes, "ffn_routes": ffn_routes, "attn_gain": attn_gain, "ffn_gain": ffn_gain, "attn_mix": attn_mix, "query_weight": query_weight, "kv_weight": kv_weight, "out_weight": out_weight, "ffn_mix": ffn_mix, "in_weight": in_weight, "down_weight": down_weight}


EPS = 1e-06
THETA = 10000.0
NEGATIVE = -1e+30

def rms_scale(values, gain):
    widened = values.astype(jnp.float32)
    inverse = lax.rsqrt(lax.optimization_barrier(jnp.mean(widened * widened, axis=-1, keepdims=True)) + EPS)
    return (widened * inverse * gain).astype(jnp.bfloat16)

def segment_of(row_index, lengths):
    ends = jnp.cumsum(lengths)
    return lax.optimization_barrier(jnp.sum((row_index[:, None] >= ends[None, :]).astype(jnp.int32), axis=1))

def positions(row_index, lengths, cached):
    ends = jnp.cumsum(lengths)
    segment = lax.optimization_barrier(jnp.sum((row_index[:, None] >= ends[None, :]).astype(jnp.int32), axis=1))
    matched = segment[:, None] == jnp.arange(lengths.shape[0], dtype=jnp.int32)[None, :]
    begins = lax.optimization_barrier(jnp.sum(jnp.where(matched, (ends - lengths)[None, :], 0), axis=1))
    offsets = lax.optimization_barrier(jnp.sum(jnp.where(matched, cached[None, :], 0), axis=1))
    return (segment, offsets + row_index - begins)

def rotate(values, place):
    half_dim = values.shape[-1] // 2
    freq = THETA ** (-jnp.arange(half_dim, dtype=jnp.float32) / half_dim)
    angle = place.astype(jnp.float32)[:, None] * freq[None, :]
    shape = (values.shape[0],) + (1,) * (values.ndim - 2) + (half_dim,)
    cosine = jnp.cos(angle).reshape(shape)
    sine = jnp.sin(angle).reshape(shape)
    former = values[..., :half_dim]
    latter = values[..., half_dim:]
    return jnp.concatenate([former * cosine - latter * sine, latter * cosine + former * sine], axis=-1)

def route_gates(normed, mixing, routes):
    logits = jnp.dot(normed, mixing, preferred_element_type=jnp.float32)
    chosen = jnp.take_along_axis(logits, routes, axis=1)
    leading = jax.nn.sigmoid(chosen[:, 0] - chosen[:, 1])
    return jnp.stack([leading, 1.0 - leading], axis=1)

def head_attention(query, key, value, allowed):
    scale = query.shape[-1] ** (-0.5)
    scores = jnp.dot(query, key.T, preferred_element_type=jnp.float32) * scale
    scores = jnp.where(allowed, scores, NEGATIVE)
    row_top = lax.optimization_barrier(jnp.max(scores, axis=1, keepdims=True))
    weights = jnp.where(allowed, jnp.exp(scores - row_top), 0.0)
    row_total = lax.optimization_barrier(jnp.sum(weights, axis=1, keepdims=True))
    mixed = jnp.dot(weights.astype(jnp.bfloat16), value, preferred_element_type=jnp.float32)
    return (mixed / row_total).astype(jnp.bfloat16)

def attention_part(tokens, lengths, cached, cache, routes, gain, mixing, query_weight, kv_weight, out_weight):
    normed = rms_scale(tokens, gain)
    row_index = jnp.arange(PACK, dtype=jnp.int32)
    segment, place = positions(row_index, lengths, cached)
    gates = route_gates(normed, mixing, routes)
    query_all = jnp.dot(normed, query_weight.reshape(D, -1), preferred_element_type=jnp.float32)
    query_all = query_all.reshape(PACK, ATT_EXPERTS, HEADS, HEAD_DIM)
    query = jnp.take_along_axis(query_all, routes[:, :, None, None], axis=1)
    query = rotate(query, place).astype(jnp.bfloat16)
    projected = jnp.dot(normed, kv_weight.reshape(D, -1), preferred_element_type=jnp.float32)
    projected = projected.reshape(PACK, 2, HEADS, HEAD_DIM)
    fresh_keys = rotate(projected[:, 0], place).astype(jnp.bfloat16)
    fresh_values = projected[:, 1].astype(jnp.bfloat16)
    stored = cache.reshape(CACHE, 2, HEADS, HEAD_DIM)
    keys = jnp.concatenate([stored[:, 0], fresh_keys], axis=0)
    values = jnp.concatenate([stored[:, 1], fresh_values], axis=0)
    cache_segment = segment_of(jnp.arange(CACHE, dtype=jnp.int32), cached)
    key_segment = jnp.concatenate([cache_segment, segment])
    key_index = jnp.concatenate([jnp.full((CACHE,), -1, jnp.int32), row_index])
    query_segment = jnp.repeat(segment, 2)
    query_index = jnp.repeat(row_index, 2)
    allowed = (query_segment[:, None] == key_segment[None, :]) & (key_index[None, :] <= query_index[:, None])
    heads = lax.map(lambda trio: head_attention(trio[0], trio[1], trio[2], allowed), (query.reshape(PACK * 2, HEADS, HEAD_DIM).transpose(1, 0, 2), keys.transpose(1, 0, 2), values.transpose(1, 0, 2)))
    attended = heads.transpose(1, 0, 2).reshape(PACK, 2, HEADS * HEAD_DIM)
    select = (routes[:, :, None] == jnp.arange(ATT_EXPERTS, dtype=jnp.int32)[None, None, :]).astype(jnp.float32)
    select = select * gates[:, :, None]
    spread = jnp.einsum('tka,tkd->tad', select, attended.astype(jnp.float32)).astype(jnp.bfloat16)
    term = jnp.dot(spread.reshape(PACK, -1), out_weight.reshape(-1, D), preferred_element_type=jnp.float32)
    return (tokens.astype(jnp.float32) + term).astype(jnp.bfloat16)

def expert_ffn(rows, in_single, down_single):
    both = jnp.dot(rows, in_single.reshape(D, 2 * FF), preferred_element_type=jnp.float32).reshape(-1, 2, FF)
    hidden = (jax.nn.silu(both[:, 0]) * both[:, 1]).astype(jnp.bfloat16)
    grouped = hidden.reshape(-1, N_SEQ, FF_GROUP).astype(jnp.float32)
    weights = down_single.reshape(N_SEQ, FF_GROUP, D).astype(jnp.float32)
    parts = jnp.einsum('rgf,gfd->rgd', grouped, weights)
    rounded = lax.optimization_barrier(parts.astype(jnp.bfloat16)).astype(jnp.float32)
    return lax.optimization_barrier(jnp.sum(rounded, axis=1))

def ffn_part(middle, routes, gain, mixing, in_weight, down_weight):
    normed = rms_scale(middle, gain)
    gates = route_gates(normed, mixing, routes).reshape(-1)
    flat = routes.reshape(-1)
    bound = min(PACK, PACK // ROWS_FFN * CAP)

    def one_expert(running, packed):
        expert, in_single, down_single = packed
        picked = jnp.nonzero(flat == expert, size=bound, fill_value=2 * PACK)[0].astype(jnp.int32)
        token = (picked // 2).astype(jnp.int32)
        rows = jnp.take(normed, token, axis=0, mode='fill', fill_value=0)
        result = expert_ffn(rows, in_single, down_single)
        weight = jnp.take(gates, picked, mode='fill', fill_value=0.0)
        return (running.at[token].add(weight[:, None] * result, mode='drop'), None)
    mixture, _ = lax.scan(one_expert, jnp.zeros((PACK, D), jnp.float32), (jnp.arange(EXPERTS, dtype=jnp.int32), in_weight, down_weight))
    return (middle.astype(jnp.float32) + mixture).astype(jnp.bfloat16)

def reference(tokens, prompt_lengths, cache_lengths, kv_cache, attn_routes, ffn_routes, attn_gain, ffn_gain, attn_mix, query_weight, kv_weight, out_weight, ffn_mix, in_weight, down_weight):
    finished = []
    for batch in range(MICRO):
        middle = attention_part(tokens[batch], prompt_lengths[batch], cache_lengths[batch], kv_cache[batch], attn_routes[batch], attn_gain, attn_mix, query_weight, kv_weight, out_weight)
        finished.append(ffn_part(middle, ffn_routes[batch], ffn_gain, ffn_mix, in_weight, down_weight))
    return jnp.stack(finished)
```

```python
import jax
import jax.numpy as jnp
from jax import lax
from jax.sharding import PartitionSpec as P

HEAD_DIM = 128


EPS = 1e-06
THETA = 10000.0
NEGATIVE = -1e30


def rms_scale(values, gain):
    widened = values.astype(jnp.float32)
    inverse = lax.rsqrt(jnp.mean(widened * widened, axis=-1, keepdims=True) + EPS)
    return (widened * inverse * gain).astype(jnp.bfloat16)


def segment_of(row_index, lengths):
    ends = jnp.cumsum(lengths)
    return jnp.sum((row_index[:, None] >= ends[None, :]).astype(jnp.int32), axis=1)


def positions(row_index, lengths, cached):
    ends = jnp.cumsum(lengths)
    segment = jnp.sum((row_index[:, None] >= ends[None, :]).astype(jnp.int32), axis=1)
    matched = segment[:, None] == jnp.arange(lengths.shape[0], dtype=jnp.int32)[None, :]
    begins = jnp.sum(jnp.where(matched, (ends - lengths)[None, :], 0), axis=1)
    offsets = jnp.sum(jnp.where(matched, cached[None, :], 0), axis=1)
    return (segment, offsets + row_index - begins)


def rotate(values, place):
    half_dim = values.shape[-1] // 2
    freq = THETA ** (-jnp.arange(half_dim, dtype=jnp.float32) / half_dim)
    angle = place.astype(jnp.float32)[:, None] * freq[None, :]
    shape = (values.shape[0],) + (1,) * (values.ndim - 2) + (half_dim,)
    cosine = jnp.cos(angle).reshape(shape)
    sine = jnp.sin(angle).reshape(shape)
    former = values[..., :half_dim]
    latter = values[..., half_dim:]
    return jnp.concatenate(
        [former * cosine - latter * sine, latter * cosine + former * sine], axis=-1
    )


def route_gates(normed, mixing, routes):
    logits = jnp.dot(normed, mixing, preferred_element_type=jnp.float32)
    chosen = jnp.take_along_axis(logits, routes, axis=1)
    leading = jax.nn.sigmoid(chosen[:, 0] - chosen[:, 1])
    return jnp.stack([leading, 1.0 - leading], axis=1)


def select_batch(values, batch):
    return lax.dynamic_index_in_dim(values, batch, 0, keepdims=False)


def attention_block(
    own_rows, lengths, cached, cache_rows, routes, gain, mixing, query_weight, kv_weight, out_weight
):
    gathered = lax.all_gather(own_rows, "expert", axis=0, tiled=True)
    count = gathered.shape[0]
    normed = rms_scale(gathered, gain)
    row_index = lax.axis_index("seq") * count + jnp.arange(count, dtype=jnp.int32)
    segment, place = positions(row_index, lengths, cached)
    gates = route_gates(normed, mixing, routes)
    experts = query_weight.shape[1]
    width = query_weight.shape[2]
    local_heads = width // HEAD_DIM
    query_all = jnp.dot(
        normed, query_weight.reshape(query_weight.shape[0], -1), preferred_element_type=jnp.float32
    )
    query_all = query_all.reshape(count, experts, local_heads, HEAD_DIM)
    query = jnp.take_along_axis(query_all, routes[:, :, None, None], axis=1)
    query = rotate(query, place).astype(jnp.bfloat16)
    queries = query.reshape(count * 2, local_heads, HEAD_DIM)
    projected = jnp.dot(
        normed, kv_weight.reshape(kv_weight.shape[0], -1), preferred_element_type=jnp.float32
    )
    projected = projected.reshape(count, 2, local_heads, HEAD_DIM)
    fresh_keys = rotate(projected[:, 0], place).astype(jnp.bfloat16).reshape(count, width)
    fresh_values = projected[:, 1].astype(jnp.bfloat16).reshape(count, width)
    fresh = jnp.stack([fresh_keys, fresh_values], axis=1)
    query_segment = jnp.repeat(segment, 2)
    query_index = jnp.repeat(row_index, 2)
    scale = HEAD_DIM ** (-0.5)
    slots = count * 2

    def absorb(carried, piece, allowed):
        row_top, row_total, row_sum = carried
        keys = piece[:, 0].reshape(-1, local_heads, HEAD_DIM)
        values = piece[:, 1].reshape(-1, local_heads, HEAD_DIM)
        scores = (
            jnp.einsum("qhd,khd->hqk", queries, keys, preferred_element_type=jnp.float32) * scale
        )
        scores = jnp.where(allowed[None], scores, NEGATIVE)
        new_top = jnp.maximum(row_top, jnp.max(scores, axis=2))
        weights = jnp.where(allowed[None], jnp.exp(scores - new_top[:, :, None]), 0.0)
        shrink = jnp.exp(row_top - new_top)
        row_total = row_total * shrink + jnp.sum(weights, axis=2)
        row_sum = row_sum * shrink[:, :, None] + jnp.einsum(
            "hqk,khd->hqd", weights.astype(jnp.bfloat16), values, preferred_element_type=jnp.float32
        )
        return (new_top, row_total, row_sum)

    initial = (
        jnp.full((local_heads, slots), NEGATIVE, jnp.float32),
        jnp.zeros((local_heads, slots), jnp.float32),
        jnp.zeros((local_heads, slots, HEAD_DIM), jnp.float32),
    )
    piece = lax.all_gather(cache_rows, "seq", axis=0, tiled=True)
    key_segment = segment_of(jnp.arange(piece.shape[0], dtype=jnp.int32), cached)
    allowed = query_segment[:, None] == key_segment[None, :]
    carried = absorb(initial, piece, allowed)
    piece = lax.all_gather(fresh, "seq", axis=0, tiled=True)
    key_index = jnp.arange(piece.shape[0], dtype=jnp.int32)
    key_segment = segment_of(key_index, lengths)
    allowed = (query_segment[:, None] == key_segment[None, :]) & (
        key_index[None, :] <= query_index[:, None]
    )
    row_top, row_total, row_sum = absorb(carried, piece, allowed)
    attended = (row_sum / row_total[:, :, None]).astype(jnp.bfloat16)
    attended = attended.transpose(1, 0, 2).reshape(count, 2, width)
    select = (routes[:, :, None] == jnp.arange(experts, dtype=jnp.int32)[None, None, :]).astype(
        jnp.float32
    )
    select = select * gates[:, :, None]
    spread = jnp.einsum("tka,tkd->tad", select, attended.astype(jnp.float32)).astype(jnp.bfloat16)
    spread = spread.reshape(count, experts * width)
    out_flat = out_weight.reshape(experts * width, -1)
    term = lax.psum_scatter(
        jnp.dot(spread, out_flat, preferred_element_type=jnp.float32).astype(jnp.bfloat16),
        "expert",
        scatter_dimension=0,
        tiled=True,
    ).astype(jnp.float32)
    return (own_rows.astype(jnp.float32) + term).astype(jnp.bfloat16)


def expert_hidden(rows, in_weight):
    single = in_weight[0]
    both = jnp.dot(rows, single.reshape(single.shape[0], -1), preferred_element_type=jnp.float32)
    both = both.reshape(rows.shape[0], 2, -1)
    return (jax.nn.silu(both[:, 0]) * both[:, 1]).astype(jnp.bfloat16)


def expert_block(middle, routes, gain, mixing, in_weight, down_weight):
    rows = middle.shape[0]
    features = middle.shape[1]
    normed = rms_scale(middle, gain)
    gates = route_gates(normed, mixing, routes)
    experts = mixing.shape[1]
    capacity = max(2, 4 * rows // experts)
    flat = routes.reshape(-1)
    member = (flat[:, None] == jnp.arange(experts, dtype=jnp.int32)[None, :]).astype(jnp.int32)
    earlier = jnp.cumsum(member, axis=0) - member
    slot = jnp.sum(earlier * member, axis=1)
    target = flat * capacity + slot
    table = (jnp.arange(experts * capacity, dtype=jnp.int32)[:, None] == target[None, :]).astype(
        jnp.bfloat16
    )
    table = jnp.sum(table.reshape(experts * capacity, rows, 2), axis=2)
    buffer = jnp.dot(table, normed, preferred_element_type=jnp.float32).astype(jnp.bfloat16)
    buffer = buffer.reshape(experts, capacity, features)
    seq_count = lax.axis_size("seq")
    copies = jnp.broadcast_to(buffer[None], (seq_count,) + buffer.shape)
    copies = copies.reshape(seq_count * experts, capacity, features)
    arrived = lax.all_to_all(copies, ("seq", "expert"), split_axis=0, concat_axis=0, tiled=True)
    flat_rows = arrived.reshape(-1, features)
    hidden = expert_hidden(flat_rows, in_weight)
    partial_value = jnp.dot(hidden, down_weight[0], preferred_element_type=jnp.float32)
    partial_value = partial_value.astype(jnp.bfloat16).reshape(arrived.shape)
    returned = lax.all_to_all(
        partial_value, ("seq", "expert"), split_axis=0, concat_axis=0, tiled=True
    )
    results = jnp.sum(
        returned.reshape(seq_count, experts, capacity, features).astype(jnp.float32), axis=0
    )
    picked = jnp.take(results.reshape(experts * capacity, features), target, axis=0).reshape(
        rows, 2, features
    )
    mixture = gates[:, 0:1] * picked[:, 0] + gates[:, 1:2] * picked[:, 1]
    return (middle.astype(jnp.float32) + mixture).astype(jnp.bfloat16)


def on_device(
    tokens,
    prompt_lengths,
    cache_lengths,
    kv_cache,
    attn_routes,
    ffn_routes,
    attn_gain,
    ffn_gain,
    attn_mix,
    query_weight,
    kv_weight,
    out_weight,
    ffn_mix,
    in_weight,
    down_weight,
):
    batch = lax.axis_index("section")
    middle = attention_block(
        select_batch(tokens, batch),
        select_batch(prompt_lengths, batch),
        select_batch(cache_lengths, batch),
        select_batch(kv_cache, batch),
        select_batch(attn_routes, batch),
        attn_gain,
        attn_mix,
        query_weight,
        kv_weight,
        out_weight,
    )
    finished = expert_block(
        middle, select_batch(ffn_routes, batch), ffn_gain, ffn_mix, in_weight, down_weight
    )
    return finished[None]


def solution(mesh):
    return jax.shard_map(
        on_device,
        mesh=mesh,
        in_specs=(
            P(None, ("seq", "expert"), None),
            P(),
            P(),
            P(None, "seq", None, "expert"),
            P(None, "seq", None),
            P(None, ("seq", "expert"), None),
            P(),
            P(),
            P(),
            P(None, None, "expert"),
            P(None, None, "expert"),
            P(None, "expert", None),
            P(),
            P("expert", None, None, "seq"),
            P("expert", "seq", None),
        ),
        out_specs=P("section", ("seq", "expert"), None),
        check_vma=False,
    )
```

```python
import math

import jax
import jax.numpy as jnp
from jax import lax
from jax.experimental import pallas as pl
from jax.experimental.pallas import tpu as pltpu
from jax.sharding import PartitionSpec as P

HEAD_DIM = 128


EPS = 1e-06
THETA = 10000.0
NEGATIVE = -1e30


def rms_scale(values, gain):
    widened = values.astype(jnp.float32)
    inverse = lax.rsqrt(jnp.mean(widened * widened, axis=-1, keepdims=True) + EPS)
    return (widened * inverse * gain).astype(jnp.bfloat16)


def route_gates(normed, mixing, routes):
    logits = jnp.dot(normed, mixing, preferred_element_type=jnp.float32)
    chosen = jnp.take_along_axis(logits, routes, axis=1)
    leading = jax.nn.sigmoid(chosen[:, 0] - chosen[:, 1])
    return jnp.stack([leading, 1.0 - leading], axis=1)


def select_batch(values, batch):
    return lax.dynamic_index_in_dim(values, batch, 0, keepdims=False)


MESH_ID = pl.DeviceIdType.MESH
NT = (((1,), (1,)), ((), ()))


def send(src, dst, sends, recvs, index, device):
    return pltpu.make_async_remote_copy(
        src_ref=src,
        dst_ref=dst,
        send_sem=sends.at[index],
        recv_sem=recvs.at[index],
        device_id=device,
        device_id_type=MESH_ID,
    )


def iota(shape, dim):
    return lax.broadcasted_iota(jnp.int32, shape, dim)


def untangle(groups):
    per = 256 // groups
    row, column = iota((256, 256), 0), iota((256, 256), 1)
    source = lax.rem(row, per) * groups + row // per
    return (column == source).astype(jnp.bfloat16)


def as_column(line, count):
    square = jnp.broadcast_to(line, (count, count))
    kept = jnp.where(iota((count, count), 0) == iota((count, count), 1), square, 0.0)
    return jnp.sum(kept, axis=1, keepdims=True)


class Spread:
    def __init__(self, buffer, sends, recvs, section, seq, expert):
        self.buffer, self.sends, self.recvs = buffer, sends, recvs
        self.near = seq
        self.right = lax.rem(seq + 2, 8)
        self.left = lax.rem(seq + 6, 8)
        self.across = seq + 1 - 2 * lax.rem(seq, 2)
        self.place = lambda other: (section, other, expert)
        right_across = lax.rem(self.across + 2, 8)
        self.copies = [
            self.copy(seq, self.across, 0),
            self.copy(seq, self.right, 1),
            self.copy(seq, self.left, 2),
            self.copy(self.across, self.right, 3),
            self.copy(self.across, self.left, 4),
            self.copy(self.left, self.right, 5),
            self.copy(right_across, self.left, 6),
        ]

    def copy(self, block, target, index):
        ref = self.buffer.at[block]
        return send(ref, ref, self.sends, self.recvs, index, self.place(target))

    def first(self):
        for index in (1, 2, 0):
            self.copies[index].start()

    def second(self):
        self.copies[0].wait_recv()
        self.copies[3].start()
        self.copies[4].start()

    def third(self):
        self.copies[1].wait_recv()
        self.copies[5].start()
        self.copies[4].wait_recv()
        self.copies[6].start()

    def finish(self):
        for index in (2, 3, 5, 6):
            self.copies[index].wait_recv()

    def drain(self):
        for index in range(7):
            self.copies[index].wait_send()


def attention_kernel(
    lengths_ref,
    cached_ref,
    tokens_ref,
    routes_ref,
    gain_ref,
    mix_ref,
    cache_hbm,
    query_hbm,
    kv_hbm,
    out_hbm,
    middle_ref,
    raw_cache,
    raw_query,
    raw_kv,
    weights,
    out_weights,
    normed,
    projected,
    cache_all,
    fresh_all,
    queries,
    top,
    total,
    summed,
    partial,
    arrived,
    load_sems,
    token_sends,
    token_recvs,
    cache_sends,
    cache_recvs,
    fresh_sends,
    fresh_recvs,
    part_sends,
    part_recvs,
):
    section = lax.axis_index("section")
    seq = lax.axis_index("seq")
    expert = lax.axis_index("expert")
    own_x = seq // 2
    loads = [
        pltpu.make_async_copy(cache_hbm.at[section], raw_cache, load_sems.at[0]),
        pltpu.make_async_copy(kv_hbm, raw_kv, load_sems.at[1]),
        pltpu.make_async_copy(query_hbm, raw_query, load_sems.at[2]),
        pltpu.make_async_copy(out_hbm, out_weights, load_sems.at[3]),
    ]
    for load in loads:
        load.start()

    caches = Spread(cache_all, cache_sends, cache_recvs, section, seq, expert)
    freshes = Spread(fresh_all, fresh_sends, fresh_recvs, section, seq, expert)
    barrier = pltpu.get_barrier_semaphore()
    for other in (caches.right, caches.left, caches.across):
        pl.semaphore_signal(
            barrier, inc=1, device_id=(section, other, expert), device_id_type=MESH_ID
        )
    for step in range(1, 8):
        peer = lax.rem(expert + step, 8)
        pl.semaphore_signal(barrier, inc=1, device_id=(section, seq, peer), device_id_type=MESH_ID)

    rows = tokens_ref[section].astype(jnp.float32)
    inverse = lax.rsqrt(jnp.mean(rows * rows, axis=-1, keepdims=True) + EPS)
    own_rows = pl.ds(pl.multiple_of(expert * 16, 16), 16)
    normed[own_rows, :] = (rows * inverse * gain_ref[...]).astype(jnp.bfloat16)
    pl.semaphore_wait(barrier, 10)
    token_copies = []
    for step in range(1, 8):
        peer = lax.rem(expert + step, 8)
        ref = normed.at[own_rows, :]
        copy = send(ref, ref, token_sends, token_recvs, step - 1, (section, seq, peer))
        copy.start()
        token_copies.append(copy)

    by_head = untangle(4)
    order = (0, 2, 1, 3)
    loads[0].wait()
    for step in range(4):
        block = jnp.dot(
            by_head, raw_cache[pl.ds(step * 256, 256), :], preferred_element_type=jnp.float32
        ).astype(jnp.bfloat16)
        for group in range(4):
            cache_all[seq, order[group], pl.ds(step * 64, 64), :] = block[
                group * 64 : group * 64 + 64, :
            ]
    caches.first()

    loads[1].wait()

    def kv_step(step, carried):
        base = pl.multiple_of(step * 512, 512)
        pair = jnp.concatenate(
            [raw_kv[pl.ds(base, 256), :], raw_kv[pl.ds(base + 256, 256), :]], axis=1
        )
        block = jnp.dot(by_head, pair, preferred_element_type=jnp.float32).astype(jnp.bfloat16)
        for half in range(2):
            at = pl.ds(pl.multiple_of(step * 128 + half * 64, 64), 64)
            for group in range(4):
                column = 1024 + order[group] * 128
                weights[at, column : column + 128] = block[
                    group * 64 : group * 64 + 64, half * 128 : half * 128 + 128
                ]
        return carried

    lax.fori_loop(0, 16, kv_step, 0)
    by_expert = untangle(8)
    loads[2].wait()

    def query_step(step, carried):
        base = pl.multiple_of(step * 512, 512)
        pair = jnp.concatenate(
            [raw_query[pl.ds(base, 256), :], raw_query[pl.ds(base + 256, 256), :]], axis=1
        )
        block = jnp.dot(by_expert, pair, preferred_element_type=jnp.float32).astype(jnp.bfloat16)
        for half in range(2):
            at = pl.ds(pl.multiple_of(step * 64 + half * 32, 32), 32)
            for group in range(8):
                column = (group % 4) * 256 + (group // 4) * 128
                weights[at, column : column + 128] = block[
                    group * 32 : group * 32 + 32, half * 128 : half * 128 + 128
                ]
        return carried

    lax.fori_loop(0, 32, query_step, 0)

    end_0 = lengths_ref[section, 0]
    end_1 = end_0 + lengths_ref[section, 1]
    held_0, held_1, held_2 = (cached_ref[section, prompt] for prompt in range(3))
    index = seq * 128 + iota((128, 1), 0)
    in_1, in_2 = index >= end_0, index >= end_1
    segment = in_1.astype(jnp.int32) + in_2.astype(jnp.int32)
    shift = jnp.where(in_2, held_2 - end_1, jnp.where(in_1, held_1 - end_0, held_0))
    place = (shift + index).astype(jnp.float32)
    lane = iota((1, 128), 1)
    freq = jnp.exp(lax.rem(lane, 64).astype(jnp.float32) * (-math.log(THETA) / 64))
    angle = place * freq
    cosine = jnp.cos(angle)
    sine = jnp.where(lane < 64, -1.0, 1.0) * jnp.sin(angle)

    def rope(value):
        return value * cosine + pltpu.roll(value, 64, 1) * sine

    routes = routes_ref[section].astype(jnp.float32)
    route_0 = as_column(routes[0:1, :], 128)
    route_1 = as_column(routes[1:2, :], 128)

    for copy in token_copies:
        copy.wait_recv()
    caches.second()

    def project(tile, carried):
        at = pl.ds(pl.multiple_of(tile * 256, 256), 256)
        projected[:, at] = jnp.dot(
            normed[...], weights[:, at], preferred_element_type=jnp.float32
        )
        return carried

    lax.fori_loop(4, 6, project, 0)
    for head in range(2):
        keys = projected[:, 1024 + head * 128 : 1152 + head * 128]
        fresh_all[seq, head, :, :] = rope(keys).astype(jnp.bfloat16)
        values = projected[:, 1280 + head * 128 : 1408 + head * 128]
        fresh_all[seq, 2 + head, :, :] = values.astype(jnp.bfloat16)
    freshes.first()
    lax.fori_loop(0, 4, project, 0)
    caches.third()

    logits = lax.dot_general(normed[...], mix_ref[...], NT, preferred_element_type=jnp.float32)

    def chosen_logit(route):
        chosen = jnp.where(route == 0.0, logits[:, 0:1], 0.0)
        for one in range(1, 4):
            chosen = chosen + jnp.where(route == float(one), logits[:, one : one + 1], 0.0)
        return chosen

    gate_0 = jax.nn.sigmoid(chosen_logit(route_0) - chosen_logit(route_1))
    gate_1 = 1.0 - gate_0

    for head in range(2):
        for place_of, route in ((0, route_0), (1, route_1)):
            query = jnp.zeros((128, 128), jnp.float32)
            for one in range(4):
                column = one * 256 + head * 128
                query = jnp.where(
                    route == float(one), projected[:, column : column + 128], query
                )
            queries[head, pl.ds(place_of * 128, 128), :] = rope(query).astype(jnp.bfloat16)

    top[...] = jnp.full_like(top, NEGATIVE)
    total[...] = jnp.zeros_like(total)
    summed[...] = jnp.zeros_like(summed)
    query_segment = jnp.concatenate([segment, segment], axis=0)
    query_index = jnp.concatenate([index, index], axis=0)
    scale = HEAD_DIM ** (-0.5)
    cache_1 = held_0
    cache_2 = held_0 + held_1

    def absorb(head, keys, values, allowed):
        scores = (
            lax.dot_general(queries[head], keys, NT, preferred_element_type=jnp.float32) * scale
        )
        scores = jnp.where(allowed, scores, NEGATIVE)
        old = top[head]
        new = jnp.maximum(old, jnp.max(scores, axis=1, keepdims=True))
        share = jnp.exp(scores - new[:, 0:1])
        shrink = jnp.exp(old - new)
        total[head] = total[head] * shrink + jnp.sum(share, axis=1, keepdims=True)
        summed[head] = summed[head] * shrink + jnp.dot(
            share.astype(jnp.bfloat16), values, preferred_element_type=jnp.float32
        )
        top[head] = new

    def cache_chunk(step, carried):
        first = lax.rem(own_x + step, 4) * 2
        slot = first * 256 + iota((1, 512), 1)
        key_segment = (slot >= cache_1).astype(jnp.int32) + (slot >= cache_2).astype(jnp.int32)
        allowed = query_segment == key_segment
        for head in range(2):
            keys = jnp.concatenate([cache_all[first, head], cache_all[first + 1, head]], axis=0)
            values = jnp.concatenate(
                [cache_all[first, 2 + head], cache_all[first + 1, 2 + head]], axis=0
            )
            absorb(head, keys, values, allowed)
        return carried

    def fresh_chunk(step, carried):
        first = lax.rem(own_x + step, 4) * 2
        slot = first * 128 + iota((1, 256), 1)
        key_segment = (slot >= end_0).astype(jnp.int32) + (slot >= end_1).astype(jnp.int32)
        allowed = (query_segment == key_segment) & (slot <= query_index)
        for head in range(2):
            keys = jnp.concatenate([fresh_all[first, head], fresh_all[first + 1, head]], axis=0)
            values = jnp.concatenate(
                [fresh_all[first, 2 + head], fresh_all[first + 1, 2 + head]], axis=0
            )
            absorb(head, keys, values, allowed)
        return carried

    freshes.second()
    cache_chunk(0, 0)
    caches.finish()
    freshes.third()
    lax.fori_loop(1, 4, cache_chunk, 0)
    freshes.finish()
    lax.fori_loop(0, 4, fresh_chunk, 0)

    pieces = []
    for one in range(4):
        for head in range(2):
            mixed = summed[head] / total[head]
            mixed = mixed.astype(jnp.bfloat16).astype(jnp.float32)
            piece = jnp.where(route_0 == float(one), gate_0 * mixed[0:128, :], 0.0)
            piece = piece + jnp.where(route_1 == float(one), gate_1 * mixed[128:256, :], 0.0)
            pieces.append(piece.astype(jnp.bfloat16))
    for copy in token_copies:
        copy.wait_send()
    for number, piece in enumerate(pieces):
        spread_at = pl.ds(number * 128, 128)
        normed[:, spread_at] = piece
    loads[3].wait()

    def out_tile(tile, carried):
        at = pl.ds(pl.multiple_of(tile * 256, 256), 256)
        partial[:, at] = jnp.dot(
            normed[:, 0:1024], out_weights[:, at], preferred_element_type=jnp.float32
        ).astype(jnp.bfloat16)
        return carried

    lax.fori_loop(0, 8, out_tile, 0)
    part_copies = []
    for step in range(1, 8):
        peer = lax.rem(expert + step, 8)
        copy = send(
            partial.at[pl.ds(pl.multiple_of(peer * 16, 16), 16), :],
            arrived.at[step - 1],
            part_sends,
            part_recvs,
            step - 1,
            (section, seq, peer),
        )
        copy.start()
        part_copies.append(copy)
    result = tokens_ref[section].astype(jnp.float32)
    term = partial[own_rows, :].astype(jnp.float32)
    for step, copy in enumerate(part_copies):
        copy.wait_recv()
        term = term + arrived[step].astype(jnp.float32)
    middle_ref[...] = (result + term).astype(jnp.bfloat16)
    for copy in part_copies:
        copy.wait_send()
    caches.drain()
    freshes.drain()


def attention_stage(
    tokens, lengths, cached, cache, routes, gain, mixing, query_weight, kv_weight, out_weight
):
    depth = tokens.shape[2]
    cache_rows = (
        cache.reshape(2, 256, 2, 2, 128).transpose(0, 1, 3, 2, 4).reshape(2, 1024, 128)
    )
    query_rows = (
        query_weight.reshape(2048, 4, 2, 128).transpose(0, 2, 1, 3).reshape(16384, 128)
    )
    kv_rows = kv_weight.reshape(2048, 2, 2, 128).transpose(0, 2, 1, 3).reshape(8192, 128)
    out_rows = out_weight.reshape(1024, depth)
    vmem = pl.BlockSpec(memory_space=pltpu.VMEM)
    smem = pl.BlockSpec(memory_space=pltpu.SMEM)
    hbm = pl.BlockSpec(memory_space=pl.ANY)
    dma = pltpu.SemaphoreType.DMA
    return pl.pallas_call(
        attention_kernel,
        out_shape=jax.ShapeDtypeStruct((16, depth), jnp.bfloat16),
        in_specs=[smem, smem, vmem, vmem, vmem, vmem, hbm, hbm, hbm, hbm],
        out_specs=vmem,
        scratch_shapes=[
            pltpu.VMEM((1024, 128), jnp.bfloat16),
            pltpu.VMEM((16384, 128), jnp.bfloat16),
            pltpu.VMEM((8192, 128), jnp.bfloat16),
            pltpu.VMEM((2048, 1536), jnp.bfloat16),
            pltpu.VMEM((1024, 2048), jnp.bfloat16),
            pltpu.VMEM((128, 2048), jnp.bfloat16),
            pltpu.VMEM((128, 1536), jnp.float32),
            pltpu.VMEM((8, 4, 256, 128), jnp.bfloat16),
            pltpu.VMEM((8, 4, 128, 128), jnp.bfloat16),
            pltpu.VMEM((2, 256, 128), jnp.bfloat16),
            pltpu.VMEM((2, 256, 128), jnp.float32),
            pltpu.VMEM((2, 256, 128), jnp.float32),
            pltpu.VMEM((2, 256, 128), jnp.float32),
            pltpu.VMEM((128, 2048), jnp.bfloat16),
            pltpu.VMEM((7, 16, 2048), jnp.bfloat16),
            dma((4,)),
            dma((7,)),
            dma((7,)),
            dma((7,)),
            dma((7,)),
            dma((7,)),
            dma((7,)),
            dma((7,)),
            dma((7,)),
        ],
        compiler_params=pltpu.CompilerParams(
            collective_id=0, has_side_effects=True, vmem_limit_bytes=48 << 20
        ),
    )(
        lengths,
        cached,
        tokens,
        routes.transpose(0, 2, 1),
        gain.reshape(1, depth),
        mixing.T,
        cache_rows,
        query_rows,
        kv_rows,
        out_rows,
    )


def expert_hidden(rows, in_weight):
    single = in_weight[0]
    both = jnp.dot(rows, single.reshape(single.shape[0], -1), preferred_element_type=jnp.float32)
    both = both.reshape(rows.shape[0], 2, -1)
    return (jax.nn.silu(both[:, 0]) * both[:, 1]).astype(jnp.bfloat16)


def expert_block(middle, routes, gain, mixing, in_weight, down_weight):
    rows = middle.shape[0]
    features = middle.shape[1]
    normed = rms_scale(middle, gain)
    gates = route_gates(normed, mixing, routes)
    experts = mixing.shape[1]
    capacity = max(2, 4 * rows // experts)
    flat = routes.reshape(-1)
    member = (flat[:, None] == jnp.arange(experts, dtype=jnp.int32)[None, :]).astype(jnp.int32)
    earlier = jnp.cumsum(member, axis=0) - member
    slot = jnp.sum(earlier * member, axis=1)
    target = flat * capacity + slot
    table = (jnp.arange(experts * capacity, dtype=jnp.int32)[:, None] == target[None, :]).astype(
        jnp.bfloat16
    )
    table = jnp.sum(table.reshape(experts * capacity, rows, 2), axis=2)
    buffer = jnp.dot(table, normed, preferred_element_type=jnp.float32).astype(jnp.bfloat16)
    buffer = buffer.reshape(experts, capacity, features)
    seq_count = lax.axis_size("seq")
    copies = jnp.broadcast_to(buffer[None], (seq_count,) + buffer.shape)
    copies = copies.reshape(seq_count * experts, capacity, features)
    arrived = lax.all_to_all(copies, ("seq", "expert"), split_axis=0, concat_axis=0, tiled=True)
    flat_rows = arrived.reshape(-1, features)
    hidden = expert_hidden(flat_rows, in_weight)
    partial_value = jnp.dot(hidden, down_weight[0], preferred_element_type=jnp.float32)
    partial_value = partial_value.astype(jnp.bfloat16).reshape(arrived.shape)
    returned = lax.all_to_all(
        partial_value, ("seq", "expert"), split_axis=0, concat_axis=0, tiled=True
    )
    results = jnp.sum(
        returned.reshape(seq_count, experts, capacity, features).astype(jnp.float32), axis=0
    )
    picked = jnp.take(results.reshape(experts * capacity, features), target, axis=0).reshape(
        rows, 2, features
    )
    mixture = gates[:, 0:1] * picked[:, 0] + gates[:, 1:2] * picked[:, 1]
    return (middle.astype(jnp.float32) + mixture).astype(jnp.bfloat16)


def on_device(
    tokens,
    prompt_lengths,
    cache_lengths,
    kv_cache,
    attn_routes,
    ffn_routes,
    attn_gain,
    ffn_gain,
    attn_mix,
    query_weight,
    kv_weight,
    out_weight,
    ffn_mix,
    in_weight,
    down_weight,
):
    batch = lax.axis_index("section")
    middle = attention_stage(
        tokens,
        prompt_lengths,
        cache_lengths,
        kv_cache,
        attn_routes,
        attn_gain,
        attn_mix,
        query_weight,
        kv_weight,
        out_weight,
    )
    finished = expert_block(
        middle, select_batch(ffn_routes, batch), ffn_gain, ffn_mix, in_weight, down_weight
    )
    return finished[None]


def solution(mesh):
    return jax.shard_map(
        on_device,
        mesh=mesh,
        in_specs=(
            P(None, ("seq", "expert"), None),
            P(),
            P(),
            P(None, "seq", None, "expert"),
            P(None, "seq", None),
            P(None, ("seq", "expert"), None),
            P(),
            P(),
            P(),
            P(None, None, "expert"),
            P(None, None, "expert"),
            P(None, "expert", None),
            P(),
            P("expert", None, None, "seq"),
            P("expert", "seq", None),
        ),
        out_specs=P("section", ("seq", "expert"), None),
        check_vma=False,
    )
```
